32 devices in a mesh: segment: 2 (over core), expert: 16 (over z, y, x).
Axes of the slice: x: 2, y: 2, z: 4, core: 2. Of those that a mesh axis runs over, the one named last changes fastest.
Arguments:
- act_a: bfloat16 [2, 384, 2048], P('segment', 'expert'), may hold values from -6 to 6
- route_a1: int32 [2, 384, 8], P('segment', 'expert'), may hold values from 0 to 15, all different within a row; in each aligned block of 24 rows (0 to 23, 24 to 47, ..., all dimensions but the last counted through in order) at most 16 rows name the same one
- gate_a1: float32 [2, 384, 8], P('segment', 'expert'), may hold values from 0.1 to 0.5
- act_b1: bfloat16 [2, 384, 2048], P('segment', 'expert'), may hold values from -6 to 6
- route_b1: int32 [2, 384, 8], P('segment', 'expert'), may hold values from 0 to 15, all different within a row; in each aligned block of 24 rows (0 to 23, 24 to 47, ..., all dimensions but the last counted through in order) at most 16 rows name the same one
- gate_b1: float32 [2, 384, 8], P('segment', 'expert'), may hold values from 0.1 to 0.5
- grad_b1: bfloat16 [2, 384, 2048], P('segment', 'expert'), may hold values from -6 to 6
- act_b2: bfloat16 [2, 384, 2048], P('segment', 'expert'), may hold values from -6 to 6
- route_a2: int32 [2, 384, 8], P('segment', 'expert'), may hold values from 0 to 15, all different within a row; in each aligned block of 24 rows (0 to 23, 24 to 47, ..., all dimensions but the last counted through in order) at most 16 rows name the same one
- gate_a2: float32 [2, 384, 8], P('segment', 'expert'), may hold values from 0.1 to 0.5
- route_b2: int32 [2, 384, 8], P('segment', 'expert'), may hold values from 0 to 15, all different within a row; in each aligned block of 24 rows (0 to 23, 24 to 47, ..., all dimensions but the last counted through in order) at most 16 rows name the same one
- gate_b2: float32 [2, 384, 8], P('segment', 'expert'), may hold values from 0.1 to 0.5
- enter_a: bfloat16 [384, 2048], P('expert'), may hold values from -6 to 6
- enter_grad: bfloat16 [384, 2048], P('expert'), may hold values from -6 to 6
- w_gate: bfloat16 [2, 16, 2048, 768], P('segment', 'expert'), may hold values from -0.125 to 0.125
- w_up: bfloat16 [2, 16, 2048, 768], P('segment', 'expert'), may hold values from -0.125 to 0.125
- w_down: bfloat16 [2, 16, 768, 2048], P('segment', 'expert'), may hold values from -0.21875 to 0.21875
Outputs:
- fwd_one: bfloat16 [2, 384, 2048], P('segment', 'expert')
- grad_one: bfloat16 [2, 384, 2048], P('segment', 'expert')
- fwd_two: bfloat16 [2, 384, 2048], P('segment', 'expert')
- grad_two: bfloat16 [2, 384, 2048], P('segment', 'expert')
The draws below stay inside these ranges and needn't reach their ends.
Inputs may be any that keep to these rules, and one draw needn't show every extreme that they name: `route_a1`: in each row the 8 experts differ; in the 24 rows of one device of one section no expert is named more than 16 times, a bound that some block reaches. `route_b1`: as for route_a1. `route_a2`: as for route_a1. `route_b2`: as for route_a1.
All inputs are finite; a program needn't handle non-finite values.
Results may differ from the reference program's by a relative error of at most 0.0085.
Values may be sent and summed in bfloat16 or wider, within the bound.
A program may use at most 128 MiB of HBM per device.

```python
import math
import jax
import jax.numpy as jnp
import numpy as np
from jax import lax

D = 2048
FF = 768
TOP = 8
TOK_DEV = 24
EXPERTS = 16
SEGMENTS = 2
CAP = 16
TOKENS = 384
N_EXPERT = 16


def block_scale(rng, extent, cuts, smallest, top_value):
    def one(dim, parts):
        steps = jax.random.uniform(jax.random.fold_in(jax.random.fold_in(rng, 6), dim), (parts,), jnp.float32, smallest / len(cuts), top_value / len(cuts))
        return jnp.repeat(jnp.exp(steps), extent[dim] // parts).reshape((-1,) + (1,) * (len(extent) - dim - 1))

    gain = one(*cuts[0])
    for cut in cuts[1:]:
        gain = gain * one(*cut)
    return gain


def assign_block(rng, own, number, rows, amount, top, reach, slope):
    ranking = jax.random.permutation(rng, amount)
    crowded, usual = portions_of(amount, rows * top, reach, slope, True), portions_of(amount, rows * top, reach, slope, False)
    places = jnp.arange(amount)

    def named(sizes, offset_by):
        used = int((sizes > 0).sum())
        fixed = max(1, used // 4)
        shifted = fixed + (places - fixed + offset_by * (used - fixed)) % max(1, amount - fixed)
        return jnp.zeros((amount,), jnp.int32).at[ranking[jnp.where(places < fixed, places, shifted)]].set(jnp.asarray(sizes, jnp.int32))

    sizes = jnp.where(number % 4 == 0, named(crowded, number // 4), named(usual, number - number // 4 - 1))
    mixed = jax.random.permutation(jax.random.fold_in(own, 3), amount)
    source_of, sink = mixed[0:amount // 2 * 2:2], mixed[1:amount // 2 * 2:2]
    slack = jnp.minimum(sizes[source_of] - 1, reach - sizes[sink]) // 2
    slack = jnp.where((source_of == ranking[0]) | (sink == ranking[0]) | (sizes[sink] == 0), 0, jnp.maximum(slack, 0))
    shifted = jax.random.randint(jax.random.fold_in(own, 4), (amount // 2,), 0, 1 << 20) % (slack + 1)
    sizes = sizes.at[source_of].add(-shifted).at[sink].add(shifted)
    items = jnp.searchsorted(jnp.cumsum(sizes), jnp.arange(rows * top), side="right").astype(jnp.int32)
    table = items.reshape(top, rows).T
    table = table[jax.random.permutation(jax.random.fold_in(own, 1), rows)]
    offset_by = jax.random.randint(jax.random.fold_in(own, 2), (rows, 1), 0, top)
    return jnp.take_along_axis(table, (jnp.arange(top)[None, :] + offset_by) % top, axis=1)


def portions_of(amount, total, bound, skew, full):
    loads = [(1 << 20) // math.isqrt(grade ** skew) + 1 for grade in range(1, amount + 1)]
    largest = bound if full else min(bound, max(-(-total // amount), total * loads[0] // sum(loads)))
    least = 1 if total - largest >= amount - 1 else 0
    counts, spare = [largest] + [least] * (amount - 1), total - largest - least * (amount - 1)
    while spare > 0:
        movable = [i for i in range(1, amount) if counts[i] < largest] or [i for i in range(1, amount) if counts[i] < bound]
        whole, left = sum([loads[i] for i in movable]), spare
        for i in movable:
            extra = min(bound - counts[i], max(1, left * loads[i] // whole), spare)
            counts[i] = counts[i] + extra
            spare = spare - extra
    return np.array(counts)


def gaussian(stream_key, extent, deviation, bound, split=(), held_as=jnp.bfloat16):
    level = block_scale(stream_key, extent, split, -0.22, 0.18) if split else 1.0
    drawn = jax.random.normal(stream_key, extent, jnp.float32) * deviation * level
    return jnp.minimum(jnp.maximum(drawn, -bound), bound).astype(held_as)


def setup_inputs(seed: int = 0) -> dict:
    splits = jax.random.split(jax.random.key(seed), 18)
    act_a = gaussian(splits[0], (SEGMENTS, TOKENS, D), 1.0, 6.0, ((0, 2), (1, 16)))
    route_a1_keys = jax.random.split(jax.random.fold_in(splits[1], 1), SEGMENTS * TOKENS // TOK_DEV)
    route_a1_turns = jax.random.permutation(jax.random.fold_in(splits[1], 3), SEGMENTS * TOKENS // TOK_DEV)
    route_a1 = jax.vmap(lambda own, number: assign_block(jax.random.fold_in(splits[1], 2), own, number, TOK_DEV, EXPERTS, TOP, CAP, 2))(route_a1_keys, route_a1_turns).reshape((SEGMENTS, TOKENS, TOP))
    gate_a1 = jnp.clip(0.1 + 0.4 * jax.random.uniform(splits[2], (SEGMENTS, TOKENS, TOP), jnp.float32) ** block_scale(splits[2], (SEGMENTS, TOKENS, TOP), ((0, 2), (1, 16)), -0.2, 0.2), 0.1, 0.5)
    act_b1 = gaussian(splits[3], (SEGMENTS, TOKENS, D), 1.0, 6.0, ((0, 2), (1, 16)))
    route_b1_keys = jax.random.split(jax.random.fold_in(splits[4], 1), SEGMENTS * TOKENS // TOK_DEV)
    route_b1_turns = jax.random.permutation(jax.random.fold_in(splits[4], 3), SEGMENTS * TOKENS // TOK_DEV)
    route_b1 = jax.vmap(lambda own, number: assign_block(jax.random.fold_in(splits[4], 2), own, number, TOK_DEV, EXPERTS, TOP, CAP, 2))(route_b1_keys, route_b1_turns).reshape((SEGMENTS, TOKENS, TOP))
    gate_b1 = jnp.clip(0.1 + 0.4 * jax.random.uniform(splits[5], (SEGMENTS, TOKENS, TOP), jnp.float32) ** block_scale(splits[5], (SEGMENTS, TOKENS, TOP), ((0, 2), (1, 16)), -0.2, 0.2), 0.1, 0.5)
    grad_b1 = gaussian(splits[6], (SEGMENTS, TOKENS, D), 1.0, 6.0, ((0, 2), (1, 16)))
    act_b2 = gaussian(splits[7], (SEGMENTS, TOKENS, D), 1.0, 6.0, ((0, 2), (1, 16)))
    route_a2_keys = jax.random.split(jax.random.fold_in(splits[8], 1), SEGMENTS * TOKENS // TOK_DEV)
    route_a2_turns = jax.random.permutation(jax.random.fold_in(splits[8], 3), SEGMENTS * TOKENS // TOK_DEV)
    route_a2 = jax.vmap(lambda own, number: assign_block(jax.random.fold_in(splits[8], 2), own, number, TOK_DEV, EXPERTS, TOP, CAP, 2))(route_a2_keys, route_a2_turns).reshape((SEGMENTS, TOKENS, TOP))
    gate_a2 = jnp.clip(0.1 + 0.4 * jax.random.uniform(splits[9], (SEGMENTS, TOKENS, TOP), jnp.float32) ** block_scale(splits[9], (SEGMENTS, TOKENS, TOP), ((0, 2), (1, 16)), -0.2, 0.2), 0.1, 0.5)
    route_b2_keys = jax.random.split(jax.random.fold_in(splits[10], 1), SEGMENTS * TOKENS // TOK_DEV)
    route_b2_turns = jax.random.permutation(jax.random.fold_in(splits[10], 3), SEGMENTS * TOKENS // TOK_DEV)
    route_b2 = jax.vmap(lambda own, number: assign_block(jax.random.fold_in(splits[10], 2), own, number, TOK_DEV, EXPERTS, TOP, CAP, 2))(route_b2_keys, route_b2_turns).reshape((SEGMENTS, TOKENS, TOP))
    gate_b2 = jnp.clip(0.1 + 0.4 * jax.random.uniform(splits[11], (SEGMENTS, TOKENS, TOP), jnp.float32) ** block_scale(splits[11], (SEGMENTS, TOKENS, TOP), ((0, 2), (1, 16)), -0.2, 0.2), 0.1, 0.5)
    enter_a = gaussian(splits[12], (TOKENS, D), 1.0, 6.0, ((0, 16),))
    enter_grad = gaussian(splits[13], (TOKENS, D), 1.0, 6.0, ((0, 16),))
    w_gate = gaussian(splits[14], (SEGMENTS, EXPERTS, D, FF), D ** -0.5, 0.125, ((0, 2), (1, 16)))
    w_up = gaussian(splits[15], (SEGMENTS, EXPERTS, D, FF), D ** -0.5, 0.125, ((0, 2), (1, 16)))
    w_down = gaussian(splits[16], (SEGMENTS, EXPERTS, FF, D), FF ** -0.5, 0.21875, ((0, 2), (1, 16)))
    return dict(act_a=act_a, route_a1=route_a1, gate_a1=gate_a1, act_b1=act_b1, route_b1=route_b1, gate_b1=gate_b1, grad_b1=grad_b1, act_b2=act_b2, route_a2=route_a2, gate_a2=gate_a2, route_b2=route_b2, gate_b2=gate_b2, enter_a=enter_a, enter_grad=enter_grad, w_gate=w_gate, w_up=w_up, w_down=w_down)


def expert_forward(inputs, gate_mat, up_mat, down_mat):
    gate_pre = jnp.dot(inputs, gate_mat, preferred_element_type=jnp.float32)
    up_pre = jnp.dot(inputs, up_mat, preferred_element_type=jnp.float32)
    hidden = (jax.nn.silu(gate_pre) * up_pre).astype(jnp.bfloat16)
    return jnp.dot(hidden, down_mat, preferred_element_type=jnp.float32).astype(jnp.bfloat16)


def expert_backward(inputs, cotangent, gate_mat, up_mat, down_mat):
    gate_pre = jnp.dot(inputs, gate_mat, preferred_element_type=jnp.float32)
    up_pre = jnp.dot(inputs, up_mat, preferred_element_type=jnp.float32)
    sigma = jax.nn.sigmoid(gate_pre)
    d_hidden = jnp.dot(cotangent, down_mat.T, preferred_element_type=jnp.float32)
    d_gate = (d_hidden * up_pre * sigma * (1.0 + gate_pre * (1.0 - sigma))).astype(jnp.bfloat16)
    d_upper = (d_hidden * gate_pre * sigma).astype(jnp.bfloat16)
    total = jnp.dot(d_gate, gate_mat.T, preferred_element_type=jnp.float32)
    total = total + jnp.dot(d_upper, up_mat.T, preferred_element_type=jnp.float32)
    return total.astype(jnp.bfloat16)


def global_slots(route):
    blocks = route.reshape(N_EXPERT, TOK_DEV * TOP)
    onehot = (blocks[:, :, None] == jnp.arange(EXPERTS, dtype=jnp.int32)[None, None, :]).astype(jnp.int32)
    before = jnp.cumsum(onehot, axis=1) - onehot
    position = jnp.sum(before * onehot, axis=2)
    source = jnp.arange(N_EXPERT, dtype=jnp.int32)[:, None]
    slots = blocks * (N_EXPERT * CAP) + source * CAP + position
    return slots.reshape(-1).astype(jnp.int32)


def dispatch(values, slots):
    buffer = jnp.zeros((EXPERTS * N_EXPERT * CAP, D), jnp.bfloat16)
    buffer = buffer.at[slots].set(jnp.repeat(values, TOP, axis=0))
    return buffer.reshape(EXPERTS, N_EXPERT * CAP, D)


def gather_back(results, slots, gates):
    picked = jnp.take(results.reshape(-1, D), slots, axis=0).astype(jnp.float32)
    picked = picked.reshape(TOKENS, TOP, D)
    return jnp.sum(picked * gates[:, :, None], axis=1).astype(jnp.bfloat16)


def layer_forward(values, route, gates, gate_all, up_all, down_all):
    slots = global_slots(route)
    buffer = dispatch(values, slots)
    results = lax.map(lambda item: expert_forward(item[0], item[1], item[2], item[3]), (buffer, gate_all, up_all, down_all))
    return gather_back(results, slots, gates)


def layer_backward(values, route, gates, cotangent, gate_all, up_all, down_all):
    slots = global_slots(route)
    buffer = dispatch(values, slots)
    cot_buffer = dispatch(cotangent, slots)
    results = lax.map(lambda item: expert_backward(item[0], item[1], item[2], item[3], item[4]), (buffer, cot_buffer, gate_all, up_all, down_all))
    return gather_back(results, slots, gates)


def reference(act_a, route_a1, gate_a1, act_b1, route_b1, gate_b1, grad_b1, act_b2, route_a2, gate_a2, route_b2, gate_b2, enter_a, enter_grad, w_gate, w_up, w_down):
    fwd_list = []
    grad_list = []
    for section in range(SEGMENTS):
        fwd_list.append(layer_forward(act_a[section], route_a1[section], gate_a1[section], w_gate[section], w_up[section], w_down[section]))
        grad_list.append(layer_backward(act_b1[section], route_b1[section], gate_b1[section], grad_b1[section], w_gate[section], w_up[section], w_down[section]))
    fwd_next = []
    grad_next = []
    for section in range(SEGMENTS):
        incoming = enter_a if section == 0 else fwd_list[section - 1]
        arriving = enter_grad if section == SEGMENTS - 1 else grad_list[section + 1]
        fwd_next.append(layer_forward(incoming, route_a2[section], gate_a2[section], w_gate[section], w_up[section], w_down[section]))
        grad_next.append(layer_backward(act_b2[section], route_b2[section], gate_b2[section], arriving, w_gate[section], w_up[section], w_down[section]))
    return (jnp.stack(fwd_list), jnp.stack(grad_list), jnp.stack(fwd_next), jnp.stack(grad_next))
```

```python
import jax
import jax.numpy as jnp
from jax import lax
from jax.sharding import PartitionSpec as P


def expert_forward(inputs, weight, gate_mat, up_mat, down_mat):
    gate_pre = jnp.dot(inputs, gate_mat, preferred_element_type=jnp.float32)
    up_pre = jnp.dot(inputs, up_mat, preferred_element_type=jnp.float32)
    hidden = (jax.nn.silu(gate_pre) * up_pre).astype(jnp.bfloat16)
    out = jnp.dot(hidden, down_mat, preferred_element_type=jnp.float32)
    return (out * weight[:, None]).astype(jnp.bfloat16)


def expert_backward(inputs, cotangent, weight, gate_mat, up_mat, down_mat):
    gate_pre = jnp.dot(inputs, gate_mat, preferred_element_type=jnp.float32)
    up_pre = jnp.dot(inputs, up_mat, preferred_element_type=jnp.float32)
    sigma = jax.nn.sigmoid(gate_pre)
    d_hidden = lax.dot_general(
        cotangent, down_mat, (((1,), (1,)), ((), ())), preferred_element_type=jnp.float32
    )
    d_gate = (d_hidden * up_pre * sigma * (1.0 + gate_pre * (1.0 - sigma))).astype(jnp.bfloat16)
    d_upper = (d_hidden * gate_pre * sigma).astype(jnp.bfloat16)
    dims = (((1,), (1,)), ((), ()))
    total = lax.dot_general(d_gate, gate_mat, dims, preferred_element_type=jnp.float32)
    total = total + lax.dot_general(d_upper, up_mat, dims, preferred_element_type=jnp.float32)
    return (total * weight[:, None]).astype(jnp.bfloat16)


def dense_gates(route, gates, experts):
    hit = route[:, :, None] == jnp.arange(experts, dtype=jnp.int32)[None, None, :]
    return jnp.sum(jnp.where(hit, gates[:, :, None], 0.0), axis=1)


def gather(block):
    return lax.all_gather(block, "expert", axis=0, tiled=True)


def scatter(block):
    return lax.psum_scatter(block, "expert", scatter_dimension=0, tiled=True)


def shards(
    act_a, route_a1, gate_a1, act_b1, route_b1, gate_b1, grad_b1, act_b2,
    route_a2, gate_a2, route_b2, gate_b2, enter_a, enter_grad, w_gate, w_up, w_down,
):
    experts = lax.axis_size("expert")
    sections = lax.axis_size("segment")
    section = lax.axis_index("segment")
    mine = lax.axis_index("expert")
    mats = (w_gate[0, 0], w_up[0, 0], w_down[0, 0])

    local = jnp.stack(
        [
            dense_gates(r[0], g[0], experts)
            for r, g in (
                (route_a1, gate_a1), (route_b1, gate_b1), (route_a2, gate_a2), (route_b2, gate_b2)
            )
        ],
        axis=0,
    )
    every = lax.all_gather(local, "expert", axis=1, tiled=True)
    weight = lax.dynamic_index_in_dim(every, mine, axis=2, keepdims=False)
    wa1, wb1, wa2, wb2 = weight[0], weight[1], weight[2], weight[3]

    x_a1 = gather(act_a[0])
    x_b1 = gather(act_b1[0])
    c_b1 = gather(grad_b1[0])
    x_b2 = gather(act_b2[0])

    fwd_one = scatter(expert_forward(x_a1, wa1, *mats))
    grad_one = scatter(expert_backward(x_b1, c_b1, wb1, *mats))

    if sections == 2:
        first = section == 0
        early = gather(jnp.where(first, enter_a, enter_grad))
        moved = lax.ppermute(jnp.where(first, fwd_one, grad_one), "segment", [(0, 1), (1, 0)])
        late = gather(moved)
        x_a2 = jnp.where(first, early, late)
        c_b2 = jnp.where(first, late, early)
    else:
        up = [(i, i + 1) for i in range(sections - 1)]
        down = [(i + 1, i) for i in range(sections - 1)]
        moved_fwd = lax.ppermute(fwd_one, "segment", up)
        moved_grad = lax.ppermute(grad_one, "segment", down)
        x_a2 = gather(jnp.where(section == 0, enter_a, moved_fwd))
        c_b2 = gather(jnp.where(section == sections - 1, enter_grad, moved_grad))

    fwd_two = scatter(expert_forward(x_a2, wa2, *mats))
    grad_two = scatter(expert_backward(x_b2, c_b2, wb2, *mats))
    return (fwd_one[None], grad_one[None], fwd_two[None], grad_two[None])


def solution(mesh):
    split = P("segment", "expert", None)
    weights = P("segment", "expert", None, None)
    in_specs = (split,) * 12 + (P("expert", None),) * 2 + (weights,) * 3
    out_specs = (split,) * 4
    return jax.shard_map(shards, mesh=mesh, in_specs=in_specs, out_specs=out_specs, check_vma=False)
```

```python
import jax
import jax.numpy as jnp
from jax import lax
from jax.experimental import pallas as pl
from jax.experimental.pallas import tpu as pltpu
from jax.sharding import PartitionSpec as P

TOP = 8


def from_behind(block, axis, distance):
    devices = range(lax.axis_size(axis))
    route = [(i - distance, i) for i in devices if i - distance in devices]
    return lax.ppermute(block, axis, route)


def expert_forward(inputs, gate_mat, up_mat, down_mat):
    gate_pre = jnp.dot(inputs, gate_mat, preferred_element_type=jnp.float32)
    up_pre = jnp.dot(inputs, up_mat, preferred_element_type=jnp.float32)
    hidden = (jax.nn.silu(gate_pre) * up_pre).astype(jnp.bfloat16)
    return jnp.dot(hidden, down_mat, preferred_element_type=jnp.float32).astype(jnp.bfloat16)


def expert_backward(inputs, cotangent, gate_mat, up_mat, down_mat):
    gate_pre = jnp.dot(inputs, gate_mat, preferred_element_type=jnp.float32)
    up_pre = jnp.dot(inputs, up_mat, preferred_element_type=jnp.float32)
    sigma = jax.nn.sigmoid(gate_pre)
    d_hidden = jnp.dot(cotangent, down_mat.T, preferred_element_type=jnp.float32)
    d_gate = (d_hidden * up_pre * sigma * (1.0 + gate_pre * (1.0 - sigma))).astype(jnp.bfloat16)
    d_upper = (d_hidden * gate_pre * sigma).astype(jnp.bfloat16)
    total = jnp.dot(d_gate, gate_mat.T, preferred_element_type=jnp.float32)
    total = total + jnp.dot(d_upper, up_mat.T, preferred_element_type=jnp.float32)
    return total.astype(jnp.bfloat16)


def local_slots(route, capacity, experts):
    routed = route.reshape(-1)
    onehot = (routed[:, None] == jnp.arange(experts, dtype=jnp.int32)[None, :]).astype(jnp.int32)
    before = jnp.cumsum(onehot, axis=0) - onehot
    position = jnp.sum(before * onehot, axis=1)
    return routed * capacity + position


def collect(values, slots, capacity, experts):
    tok_rows = values.shape[0]
    chosen = slots[:, None] == jnp.arange(experts * capacity, dtype=jnp.int32)[None, :]
    select = chosen.reshape(tok_rows, TOP, experts * capacity).any(axis=1).astype(jnp.bfloat16)
    packed = jnp.einsum("tj,td->jd", select, values, preferred_element_type=jnp.float32)
    return packed.astype(jnp.bfloat16).reshape(experts, capacity, values.shape[1])


def spread(returned, slots, gates):
    width = returned.shape[2]
    picked = jnp.take(returned.reshape(-1, width), slots, axis=0).astype(jnp.float32)
    picked = picked.reshape(gates.shape[0], gates.shape[1], width)
    return jnp.sum(picked * gates[:, :, None], axis=1).astype(jnp.bfloat16)


def slot_shards(
    act_a,
    route_a1,
    gate_a1,
    act_b1,
    route_b1,
    gate_b1,
    grad_b1,
    act_b2,
    route_a2,
    gate_a2,
    route_b2,
    gate_b2,
    enter_a,
    enter_grad,
    w_gate,
    w_up,
    w_down,
):
    experts = lax.axis_size("expert")
    tok_rows = act_a.shape[1]
    width = act_a.shape[2]
    capacity = 4 * tok_rows * TOP // (3 * experts)
    gate_mat = w_gate[0, 0]
    up_mat = w_up[0, 0]
    down_mat = w_down[0, 0]

    def run_forward(received):
        flat_in = received.reshape(-1, width)
        return expert_forward(flat_in, gate_mat, up_mat, down_mat).reshape(received.shape)

    def run_backward(received, cot_received):
        flat_in = received.reshape(-1, width)
        flat_cot = cot_received.reshape(-1, width)
        return expert_backward(flat_in, flat_cot, gate_mat, up_mat, down_mat).reshape(
            received.shape
        )

    def one_tick(fwd_in, fwd_route, fwd_gates, bwd_in, bwd_route, bwd_gates, bwd_cot):
        slots_fwd = local_slots(fwd_route, capacity, experts)
        slots_bwd = local_slots(bwd_route, capacity, experts)
        send_fwd = collect(fwd_in, slots_fwd, capacity, experts)
        send_inputs = collect(bwd_in, slots_bwd, capacity, experts)
        send_cot = collect(bwd_cot, slots_bwd, capacity, experts)
        back_fwd = lax.all_to_all(
            run_forward(
                lax.all_to_all(send_fwd, "expert", split_axis=0, concat_axis=0, tiled=True)
            ),
            "expert",
            split_axis=0,
            concat_axis=0,
            tiled=True,
        )
        back_bwd = lax.all_to_all(
            run_backward(
                lax.all_to_all(send_inputs, "expert", split_axis=0, concat_axis=0, tiled=True),
                lax.all_to_all(send_cot, "expert", split_axis=0, concat_axis=0, tiled=True),
            ),
            "expert",
            split_axis=0,
            concat_axis=0,
            tiled=True,
        )
        out_fwd = spread(back_fwd, slots_fwd, fwd_gates)
        out_bwd = spread(back_bwd, slots_bwd, bwd_gates)
        return (out_fwd[None], out_bwd[None])

    fwd_one, grad_one = one_tick(
        act_a[0], route_a1[0], gate_a1[0], act_b1[0], route_b1[0], gate_b1[0], grad_b1[0]
    )
    section = lax.axis_index("segment")
    moved_fwd = from_behind(fwd_one, "segment", 1)
    moved_grad = from_behind(grad_one, "segment", -1)
    in_two = jnp.where(section == 0, enter_a[None], moved_fwd)
    cot_two = jnp.where(section == lax.axis_size("segment") - 1, enter_grad[None], moved_grad)
    fwd_two, grad_two = one_tick(
        in_two[0], route_a2[0], gate_a2[0], act_b2[0], route_b2[0], gate_b2[0], cot_two[0]
    )
    return (fwd_one, grad_one, fwd_two, grad_two)


Z = 4
Q = 4
JOBS = 4
BIG = 6
TILE = 256
LANES = 128
MESH = pl.DeviceIdType.MESH
F32 = jnp.float32
BF16 = jnp.bfloat16


def nt_dot(left, right):
    return lax.dot_general(left, right, (((1,), (1,)), ((), ())), preferred_element_type=F32)


def layer_kernel(
    xs, wt, wg_h, wu_h, wd_h, out,
    gath, gath_w, part, late, wg, wu, wd, h0, h1, wcol, d0, d1, rx, ry, sums, zin,
    loc_sem, wsem, agz_s, agz_r, agl_s, agl_r, rsl_s, rsl_r, rsz_s, rsz_r, cross_s, cross_r,
):
    sec = lax.axis_index("segment")
    me = lax.axis_index("expert")
    z = me // Q
    q = me % Q
    x_pos = q % 2
    y_pos = q // 2
    qx = q + 1 - 2 * x_pos
    qy = q + 2 - 4 * y_pos
    qd = Q - 1 - q
    x_peer = z * Q + qx
    y_peer = z * Q + qy
    width = xs.shape[2]
    rows = xs.shape[1]
    total = Q * Z * rows
    half = width // 2
    lo = pl.ds(0, half)
    hi = pl.ds(half, half)
    hidden = wg.shape[1]

    def rcopy(src, dst, ssem, rsem, peer, seg=sec):
        return pltpu.make_async_remote_copy(
            src_ref=src, dst_ref=dst, send_sem=ssem, recv_sem=rsem,
            device_id=(seg, peer), device_id_type=MESH,
        )

    barrier = pltpu.get_barrier_semaphore()
    z_peers = [((z + j) % Z) * Q + q for j in range(1, Z)]
    z_from = [(z + Z - j) % Z for j in range(1, Z)]
    for peer in z_peers + [x_peer, y_peer]:
        pl.semaphore_signal(barrier, inc=1, device_id=(sec, peer), device_id_type=MESH)
    pl.semaphore_signal(barrier, inc=1, device_id=(1 - sec, me), device_id_type=MESH)

    w_copies = [
        pltpu.make_async_copy(src, dst, wsem.at[i])
        for i, (src, dst) in enumerate(((wg_h, wg), (wu_h, wu), (wd_h, wd)))
    ]
    for c in w_copies:
        c.start()

    def buf(k):
        return gath.at[k] if k < BIG else gath_w

    def src(k):
        return xs.at[k] if k < BIG - 1 else (late if k == BIG - 1 else wt)

    def own_copy(k):
        return pltpu.make_async_copy(src(k), buf(k).at[q, z], loc_sem.at[k])

    def z_send(k, j):
        return rcopy(src(k), buf(k).at[q, z], agz_s.at[k, j], agz_r.at[k, j], z_peers[j])

    def z_recv(k, j):
        return rcopy(src(k), buf(k).at[q, z_from[j]], agz_s.at[k, j], agz_r.at[k, j], z_peers[j])

    def ag_start(k):
        own_copy(k).start()
        for j in range(Z - 1):
            z_send(k, j).start()

    def lay(k, i, block, cols, peer):
        ref = buf(k).at[block] if cols is None else buf(k).at[block, :, :, cols]
        return rcopy(ref, ref, agl_s.at[k, i], agl_r.at[k, i], peer)

    def cols(k, c):
        return c if k < BIG else None

    def l1(k):
        own_copy(k).wait()
        for j in range(Z - 1):
            z_recv(k, j).wait_recv()
        lay(k, 0, q, None, x_peer).start()
        lay(k, 1, q, None, y_peer).start()

    def l2(k):
        lay(k, 0, qx, None, x_peer).wait_recv()
        lay(k, 2, qx, cols(k, lo), y_peer).start()
        lay(k, 1, qy, None, y_peer).wait_recv()
        if k < BIG:
            lay(k, 3, qy, hi, x_peer).start()

    def arrived(k):
        lay(k, 2, qd, cols(k, lo), y_peer).wait_recv()
        if k < BIG:
            lay(k, 3, qd, hi, x_peer).wait_recv()

    def ag_drain(k):
        for j in range(Z - 1):
            z_send(k, j).wait_send()
        lay(k, 0, q, None, x_peer).wait_send()
        lay(k, 1, q, None, y_peer).wait_send()
        lay(k, 2, qx, cols(k, lo), y_peer).wait_send()
        if k < BIG:
            lay(k, 3, qy, hi, x_peer).wait_send()

    def rs_copies(j):
        def one(i, s, d, peer):
            return rcopy(s, d, rsl_s.at[j, i], rsl_r.at[j, i], peer)

        return (
            one(0, part.at[j, qd, :, :, lo], d0.at[j], x_peer),
            one(1, part.at[j, qd, :, :, hi], d1.at[j], y_peer),
            one(2, part.at[j, qx], rx.at[j], x_peer),
            one(3, part.at[j, qy], ry.at[j], y_peer),
        )

    def rs_z(j, i):
        return rcopy(
            sums.at[j, z_peers[i] // Q], zin.at[j, i], rsz_s.at[j, i], rsz_r.at[j, i], z_peers[i]
        )

    def s1(j):
        a, b, _, _ = rs_copies(j)
        a.start()
        b.start()

    def s2(j):
        a, b, c, d = rs_copies(j)
        a.wait_recv()
        part[j, qy, :, :, lo] = (
            part[j, qy, :, :, lo].astype(F32) + d0[j].astype(F32)
        ).astype(BF16)
        d.start()
        b.wait_recv()
        part[j, qx, :, :, hi] = (
            part[j, qx, :, :, hi].astype(F32) + d1[j].astype(F32)
        ).astype(BF16)
        c.start()

    def s3(j):
        _, _, c, d = rs_copies(j)
        c.wait_recv()
        d.wait_recv()
        for i in range(Z - 1):
            zz = z_peers[i] // Q
            sums[j, zz] = (
                part[j, q, zz].astype(F32) + rx[j, zz].astype(F32) + ry[j, zz].astype(F32)
            ).astype(BF16)
            rs_z(j, i).start()

    def fin(j):
        for i in range(Z - 1):
            rs_z(j, i).wait_recv()
        acc = part[j, q, z].astype(F32) + rx[j, z].astype(F32) + ry[j, z].astype(F32)
        for i in range(Z - 1):
            acc = acc + zin[j, i].astype(F32)
        out[j] = acc.astype(BF16)

    def rs_drain(j):
        for c in rs_copies(j):
            c.wait_send()
        for i in range(Z - 1):
            rs_z(j, i).wait_send()

    def crossing():
        return rcopy(out.at[0], late, cross_s, cross_r, me, 1 - sec)

    def tile(n):
        return pl.ds(pl.multiple_of(n * TILE, TILE), TILE)

    def part_a(j, is_f):
        lane = lax.broadcasted_iota(jnp.int32, (total, LANES), 1)
        table = gath_w[...].reshape(total, LANES)
        picked = jnp.sum(jnp.where(lane == j * (Q * Z) + me, table, 0.0), axis=1, keepdims=True)
        wcol[...] = jnp.broadcast_to(picked, (total, LANES))

        @pl.when(is_f)
        def _():
            xi = j + (j + 1) // 2

            def body(n, carry):
                x = gath[xi].reshape(total, width)
                g = jnp.dot(x, wg[:, tile(n)], preferred_element_type=F32)
                u = jnp.dot(x, wu[:, tile(n)], preferred_element_type=F32)
                h0[:, tile(n)] = (g * jax.nn.sigmoid(g) * u).astype(BF16)
                return carry

            lax.fori_loop(0, hidden // TILE, body, 0)

        @pl.when(jnp.logical_not(is_f))
        def _():
            xi = jnp.where(j >= 2, 4, j)
            ci = j + 1 + j // 3

            def body(n, carry):
                x = gath[xi].reshape(total, width)
                c = gath[ci].reshape(total, width)
                g = jnp.dot(x, wg[:, tile(n)], preferred_element_type=F32)
                u = jnp.dot(x, wu[:, tile(n)], preferred_element_type=F32)
                dh = nt_dot(c, wd[tile(n), :])
                sig = jax.nn.sigmoid(g)
                h0[:, tile(n)] = (dh * u * sig * (1.0 + g * (1.0 - sig))).astype(BF16)
                h1[:, tile(n)] = (dh * g * sig).astype(BF16)
                return carry

            lax.fori_loop(0, hidden // TILE, body, 0)

    def part_b(j, is_f):
        def put(n, o):
            w = jnp.concatenate([wcol[...]] * (TILE // LANES), axis=1)
            part[j, :, :, :, tile(n)] = (o * w).astype(BF16).reshape(Q, Z, rows, TILE)

        @pl.when(is_f)
        def _():
            def body(n, carry):
                put(n, jnp.dot(h0[...], wd[:, tile(n)], preferred_element_type=F32))
                return carry

            lax.fori_loop(0, width // TILE, body, 0)

        @pl.when(jnp.logical_not(is_f))
        def _():
            def body(n, carry):
                put(n, nt_dot(h0[...], wg[tile(n), :]) + nt_dot(h1[...], wu[tile(n), :]))
                return carry

            lax.fori_loop(0, width // TILE, body, 0)

    pl.semaphore_wait(barrier, Z + 2)
    W = BIG
    for k in (0, 1, W, 2, 3, 4):
        ag_start(k)
    l1(0)
    l1(1)
    l1(W)
    l2(0)
    l1(2)
    l2(1)
    l2(W)
    arrived(0)
    for c in w_copies:
        c.wait()
    arrived(1)
    arrived(W)

    def mid_0():
        l2(2)
        l1(3)

    def end_0():
        s1(0)
        arrived(2)

    def mid_1():
        s2(0)
        l2(3)

    def end_1():
        s1(1)
        l1(4)
        s3(0)
        arrived(3)
        s2(1)
        l2(4)
        fin(0)
        crossing().start()
        crossing().wait_recv()
        ag_start(5)
        arrived(4)

    def mid_2():
        s3(1)
        l1(5)

    def end_2():
        s1(2)
        l2(5)
        fin(1)
        s2(2)
        arrived(5)

    def mid_3():
        s3(2)

    def end_3():
        s1(3)
        s2(3)
        fin(2)
        s3(3)
        fin(3)

    mids = (mid_0, mid_1, mid_2, mid_3)
    ends = (end_0, end_1, end_2, end_3)

    def job(j, carry):
        is_f = (sec + j) % 2 == 0
        part_a(j, is_f)
        for i, fn in enumerate(mids):
            pl.when(j == i)(fn)
        part_b(j, is_f)
        for i, fn in enumerate(ends):
            pl.when(j == i)(fn)
        return carry

    lax.fori_loop(0, JOBS, job, 0)

    for k in range(BIG + 1):
        ag_drain(k)
    for j in range(JOBS):
        rs_drain(j)
    crossing().wait_send()


def fused_shards(
    act_a, route_a1, gate_a1, act_b1, route_b1, gate_b1, grad_b1, act_b2,
    route_a2, gate_a2, route_b2, gate_b2, enter_a, enter_grad, w_gate, w_up, w_down,
):
    experts = lax.axis_size("expert")
    first = lax.axis_index("segment") == 0
    rows, width = act_a.shape[1:]
    hidden = w_gate.shape[3]

    def pick(one, two):
        return jnp.where(first, one, two)

    xs = jnp.stack(
        [
            pick(act_a[0], act_b1[0]),
            pick(act_b1[0], grad_b1[0]),
            pick(grad_b1[0], act_a[0]),
            pick(enter_a, enter_grad),
            act_b2[0],
        ],
        axis=0,
    )
    pairs = ((route_a1, gate_a1), (route_b1, gate_b1), (route_a2, gate_a2), (route_b2, gate_b2))
    route = jnp.stack([pick(pairs[j][0][0], pairs[j ^ 1][0][0]) for j in range(JOBS)], axis=1)
    gate = jnp.stack([pick(pairs[j][1][0], pairs[j ^ 1][1][0]) for j in range(JOBS)], axis=1)
    hit = route[:, :, :, None] == jnp.arange(experts, dtype=jnp.int32)
    dense = jnp.sum(jnp.where(hit, gate[:, :, :, None], 0.0), axis=2)
    wt = jnp.pad(dense.reshape(rows, JOBS * experts), ((0, 0), (0, LANES - JOBS * experts)))

    vmem = pl.BlockSpec(memory_space=pltpu.VMEM)
    hbm = pl.BlockSpec(memory_space=pl.ANY)
    dma = pltpu.SemaphoreType.DMA
    total = experts * rows
    done = pl.pallas_call(
        layer_kernel,
        out_shape=jax.ShapeDtypeStruct((JOBS, rows, width), BF16),
        in_specs=[vmem, vmem, hbm, hbm, hbm],
        out_specs=vmem,
        scratch_shapes=[
            pltpu.VMEM((BIG, Q, Z, rows, width), BF16),
            pltpu.VMEM((Q, Z, rows, LANES), F32),
            pltpu.VMEM((JOBS, Q, Z, rows, width), BF16),
            pltpu.VMEM((rows, width), BF16),
            pltpu.VMEM((width, hidden), BF16),
            pltpu.VMEM((width, hidden), BF16),
            pltpu.VMEM((hidden, width), BF16),
            pltpu.VMEM((total, hidden), BF16),
            pltpu.VMEM((total, hidden), BF16),
            pltpu.VMEM((total, LANES), F32),
            pltpu.VMEM((JOBS, Z, rows, width // 2), BF16),
            pltpu.VMEM((JOBS, Z, rows, width // 2), BF16),
            pltpu.VMEM((JOBS, Z, rows, width), BF16),
            pltpu.VMEM((JOBS, Z, rows, width), BF16),
            pltpu.VMEM((JOBS, Z, rows, width), BF16),
            pltpu.VMEM((JOBS, Z - 1, rows, width), BF16),
            dma((BIG + 1,)), dma((3,)),
            dma((BIG + 1, Z - 1)), dma((BIG + 1, Z - 1)),
            dma((BIG + 1, 4)), dma((BIG + 1, 4)),
            dma((JOBS, 4)), dma((JOBS, 4)),
            dma((JOBS, Z - 1)), dma((JOBS, Z - 1)),
            dma, dma,
        ],
        compiler_params=pltpu.CompilerParams(
            collective_id=0, has_side_effects=True, vmem_limit_bytes=60 * 1024 * 1024
        ),
    )(xs, wt, w_gate[0, 0], w_up[0, 0], w_down[0, 0])
    fwd_one, grad_one = pick(done[0], done[1]), pick(done[1], done[0])
    fwd_two, grad_two = pick(done[2], done[3]), pick(done[3], done[2])
    return (fwd_one[None], grad_one[None], fwd_two[None], grad_two[None])


def solution(mesh):
    split = P("segment", "expert", None)
    weights = P("segment", "expert", None, None)
    in_specs = (split,) * 12 + (P("expert", None),) * 2 + (weights,) * 3
    out_specs = (split,) * 4
    fits = mesh.shape["segment"] == 2 and mesh.shape["expert"] == Q * Z
    body = fused_shards if fits else slot_shards
    return jax.shard_map(body, mesh=mesh, in_specs=in_specs, out_specs=out_specs, check_vma=False)
```

```python
import jax
import jax.numpy as jnp
from jax import lax
from jax.experimental import pallas as pl
from jax.experimental.pallas import tpu as pltpu
from jax.sharding import PartitionSpec as P

TOP = 8


def from_behind(block, axis, distance):
    devices = range(lax.axis_size(axis))
    route = [(i - distance, i) for i in devices if i - distance in devices]
    return lax.ppermute(block, axis, route)


def expert_forward(inputs, gate_mat, up_mat, down_mat):
    gate_pre = jnp.dot(inputs, gate_mat, preferred_element_type=jnp.float32)
    up_pre = jnp.dot(inputs, up_mat, preferred_element_type=jnp.float32)
    hidden = (jax.nn.silu(gate_pre) * up_pre).astype(jnp.bfloat16)
    return jnp.dot(hidden, down_mat, preferred_element_type=jnp.float32).astype(jnp.bfloat16)


def expert_backward(inputs, cotangent, gate_mat, up_mat, down_mat):
    gate_pre = jnp.dot(inputs, gate_mat, preferred_element_type=jnp.float32)
    up_pre = jnp.dot(inputs, up_mat, preferred_element_type=jnp.float32)
    sigma = jax.nn.sigmoid(gate_pre)
    d_hidden = jnp.dot(cotangent, down_mat.T, preferred_element_type=jnp.float32)
    d_gate = (d_hidden * up_pre * sigma * (1.0 + gate_pre * (1.0 - sigma))).astype(jnp.bfloat16)
    d_upper = (d_hidden * gate_pre * sigma).astype(jnp.bfloat16)
    total = jnp.dot(d_gate, gate_mat.T, preferred_element_type=jnp.float32)
    total = total + jnp.dot(d_upper, up_mat.T, preferred_element_type=jnp.float32)
    return total.astype(jnp.bfloat16)


def local_slots(route, capacity, experts):
    routed = route.reshape(-1)
    onehot = (routed[:, None] == jnp.arange(experts, dtype=jnp.int32)[None, :]).astype(jnp.int32)
    before = jnp.cumsum(onehot, axis=0) - onehot
    position = jnp.sum(before * onehot, axis=1)
    return routed * capacity + position


def collect(values, slots, capacity, experts):
    tok_rows = values.shape[0]
    chosen = slots[:, None] == jnp.arange(experts * capacity, dtype=jnp.int32)[None, :]
    select = chosen.reshape(tok_rows, TOP, experts * capacity).any(axis=1).astype(jnp.bfloat16)
    packed = jnp.einsum("tj,td->jd", select, values, preferred_element_type=jnp.float32)
    return packed.astype(jnp.bfloat16).reshape(experts, capacity, values.shape[1])


def spread(returned, slots, gates):
    width = returned.shape[2]
    picked = jnp.take(returned.reshape(-1, width), slots, axis=0).astype(jnp.float32)
    picked = picked.reshape(gates.shape[0], gates.shape[1], width)
    return jnp.sum(picked * gates[:, :, None], axis=1).astype(jnp.bfloat16)


def slot_shards(
    act_a,
    route_a1,
    gate_a1,
    act_b1,
    route_b1,
    gate_b1,
    grad_b1,
    act_b2,
    route_a2,
    gate_a2,
    route_b2,
    gate_b2,
    enter_a,
    enter_grad,
    w_gate,
    w_up,
    w_down,
):
    experts = lax.axis_size("expert")
    tok_rows = act_a.shape[1]
    width = act_a.shape[2]
    capacity = 4 * tok_rows * TOP // (3 * experts)
    gate_mat = w_gate[0, 0]
    up_mat = w_up[0, 0]
    down_mat = w_down[0, 0]

    def run_forward(received):
        flat_in = received.reshape(-1, width)
        return expert_forward(flat_in, gate_mat, up_mat, down_mat).reshape(received.shape)

    def run_backward(received, cot_received):
        flat_in = received.reshape(-1, width)
        flat_cot = cot_received.reshape(-1, width)
        return expert_backward(flat_in, flat_cot, gate_mat, up_mat, down_mat).reshape(
            received.shape
        )

    def one_tick(fwd_in, fwd_route, fwd_gates, bwd_in, bwd_route, bwd_gates, bwd_cot):
        slots_fwd = local_slots(fwd_route, capacity, experts)
        slots_bwd = local_slots(bwd_route, capacity, experts)
        send_fwd = collect(fwd_in, slots_fwd, capacity, experts)
        send_inputs = collect(bwd_in, slots_bwd, capacity, experts)
        send_cot = collect(bwd_cot, slots_bwd, capacity, experts)
        back_fwd = lax.all_to_all(
            run_forward(
                lax.all_to_all(send_fwd, "expert", split_axis=0, concat_axis=0, tiled=True)
            ),
            "expert",
            split_axis=0,
            concat_axis=0,
            tiled=True,
        )
        back_bwd = lax.all_to_all(
            run_backward(
                lax.all_to_all(send_inputs, "expert", split_axis=0, concat_axis=0, tiled=True),
                lax.all_to_all(send_cot, "expert", split_axis=0, concat_axis=0, tiled=True),
            ),
            "expert",
            split_axis=0,
            concat_axis=0,
            tiled=True,
        )
        out_fwd = spread(back_fwd, slots_fwd, fwd_gates)
        out_bwd = spread(back_bwd, slots_bwd, bwd_gates)
        return (out_fwd[None], out_bwd[None])

    fwd_one, grad_one = one_tick(
        act_a[0], route_a1[0], gate_a1[0], act_b1[0], route_b1[0], gate_b1[0], grad_b1[0]
    )
    section = lax.axis_index("segment")
    moved_fwd = from_behind(fwd_one, "segment", 1)
    moved_grad = from_behind(grad_one, "segment", -1)
    in_two = jnp.where(section == 0, enter_a[None], moved_fwd)
    cot_two = jnp.where(section == lax.axis_size("segment") - 1, enter_grad[None], moved_grad)
    fwd_two, grad_two = one_tick(
        in_two[0], route_a2[0], gate_a2[0], act_b2[0], route_b2[0], gate_b2[0], cot_two[0]
    )
    return (fwd_one, grad_one, fwd_two, grad_two)


Z = 4
Q = 4
JOBS = 4
BIG = 6
TILE = 256
LANES = 128
MESH = pl.DeviceIdType.MESH
F32 = jnp.float32
BF16 = jnp.bfloat16


def nt_dot(left, right):
    return lax.dot_general(left, right, (((1,), (1,)), ((), ())), preferred_element_type=F32)


def layer_kernel(
    act_a, act_b1, grad_b1, enter_a, enter_grad, act_b2,
    ra1, rb1, ra2, rb2, ga1, gb1, ga2, gb2, wg_h, wu_h, wd_h, out,
    gath, gath_w, wt, part, late, wg, wu, wd, h0, h1, wcol, d0, d1, rx, ry, sums, zin,
    loc_sem, wsem, agz_s, agz_r, agl_s, agl_r, agd_s, agd_r, rsl_s, rsl_r, rsz_s, rsz_r,
    cross_s, cross_r,
):
    sec = lax.axis_index("segment")
    me = lax.axis_index("expert")
    first = sec == 0
    z = me // Q
    q = me % Q
    x_pos = q % 2
    y_pos = q // 2
    qx = q + 1 - 2 * x_pos
    qy = q + 2 - 4 * y_pos
    qd = Q - 1 - q
    x_peer = z * Q + qx
    y_peer = z * Q + qy
    rows, width = act_a.shape
    total = Q * Z * rows
    half = width // 2
    lo = pl.ds(0, half)
    hi = pl.ds(half, half)
    hidden = wg.shape[1]
    W = BIG

    def rcopy(src, dst, ssem, rsem, peer, seg=sec):
        return pltpu.make_async_remote_copy(
            src_ref=src, dst_ref=dst, send_sem=ssem, recv_sem=rsem,
            device_id=(seg, peer), device_id_type=MESH,
        )

    barrier = pltpu.get_barrier_semaphore()
    z_peers = [((z + j) % Z) * Q + q for j in range(1, Z)]
    z_from = [(z + Z - j) % Z for j in range(1, Z)]
    for peer in z_peers + [x_peer, y_peer]:
        pl.semaphore_signal(barrier, inc=1, device_id=(sec, peer), device_id_type=MESH)
    pl.semaphore_signal(barrier, inc=1, device_id=(1 - sec, me), device_id_type=MESH)

    w_copies = [
        pltpu.make_async_copy(src, dst, wsem.at[i])
        for i, (src, dst) in enumerate(((wg_h, wg), (wu_h, wu), (wd_h, wd)))
    ]

    sources = (
        (act_a, act_b1), (act_b1, grad_b1), (grad_b1, act_a), (enter_a, enter_grad),
        (act_b2, act_b2), (late, late), (wt, wt),
    )

    def by_section(k, fn):
        one, two = sources[k]
        if one is two:
            fn(one)
        else:
            pl.when(first)(lambda: fn(one))
            pl.when(jnp.logical_not(first))(lambda: fn(two))

    def buf(k):
        return gath.at[k] if k < BIG else gath_w

    def own_copy(k, src):
        return pltpu.make_async_copy(src, buf(k).at[q, z], loc_sem.at[k])

    def z_send(k, j, src):
        return rcopy(src, buf(k).at[q, z], agz_s.at[k, j], agz_r.at[k, j], z_peers[j])

    def z_recv(k, j):
        dst = buf(k).at[q, z_from[j]]
        return rcopy(sources[k][0], dst, agz_s.at[k, j], agz_r.at[k, j], z_peers[j])

    def start_z(k):
        def go(src):
            own_copy(k, src).start()
            for j in range(Z - 1):
                z_send(k, j, src).start()

        by_section(k, go)

    def lay(k, axis, i, block, zz, src=None):
        ref = buf(k).at[block, zz]
        peer = x_peer if axis == 0 else y_peer
        return rcopy(
            ref if src is None else src, ref, agl_s.at[k, axis, i], agl_r.at[k, axis, i], peer
        )

    def start_near(k):
        def go(src):
            lay(k, 0, Z - 1, q, z, src).start()
            lay(k, 1, Z - 1, q, z, src).start()

        by_section(k, go)

    def l1(k):
        for j in range(Z - 1):
            z_recv(k, j).wait_recv()
            lay(k, 0, j, q, z_from[j]).start()
            lay(k, 1, j, q, z_from[j]).start()

    def diag(k, i, block):
        if k == W:
            ref = buf(k).at[block]
        else:
            ref = buf(k).at[block, :, :, lo if i == 0 else hi]
        return rcopy(ref, ref, agd_s.at[k, i], agd_r.at[k, i], y_peer if i == 0 else x_peer)

    def near_wait(k, axis):
        block = qx if axis == 0 else qy
        for j in range(Z - 1):
            lay(k, axis, j, block, z_from[j]).wait_recv()
        lay(k, axis, Z - 1, block, z).wait_recv()

    def l2(k):
        near_wait(k, 0)
        diag(k, 0, qx).start()
        near_wait(k, 1)
        if k != W:
            diag(k, 1, qy).start()

    def arrived(k):
        own_copy(k, sources[k][0]).wait()
        diag(k, 0, qd).wait_recv()
        if k != W:
            diag(k, 1, qd).wait_recv()

    def ag_drain(k):
        for j in range(Z - 1):
            z_send(k, j, sources[k][0]).wait_send()
            lay(k, 0, j, q, z_from[j]).wait_send()
            lay(k, 1, j, q, z_from[j]).wait_send()
        lay(k, 0, Z - 1, q, z).wait_send()
        lay(k, 1, Z - 1, q, z).wait_send()
        diag(k, 0, qx).wait_send()
        if k != W:
            diag(k, 1, qy).wait_send()

    def rs(j, i):
        s, d, peer = (
            lambda: (part.at[j, qd, :, :, lo], d0.at[j], x_peer),
            lambda: (part.at[j, qx, :, :, lo], rx.at[j, :, :, lo], x_peer),
            lambda: (part.at[j, qd, :, :, hi], d1.at[j], y_peer),
            lambda: (part.at[j, qy, :, :, hi], ry.at[j, :, :, hi], y_peer),
            lambda: (part.at[j, qy, :, :, lo], ry.at[j, :, :, lo], y_peer),
            lambda: (part.at[j, qx, :, :, hi], rx.at[j, :, :, hi], x_peer),
        )[i]()
        return rcopy(s, d, rsl_s.at[j, i], rsl_r.at[j, i], peer)

    def rs_z(j, i, h):
        c = hi if h else lo
        return rcopy(
            sums.at[j, z_peers[i] // Q, :, c], zin.at[j, i, :, c],
            rsz_s.at[j, i, h], rsz_r.at[j, i, h], z_peers[i],
        )

    def sa(j):
        rs(j, 0).start()
        rs(j, 1).start()

    def sb(j):
        rs(j, 2).start()
        rs(j, 3).start()

    def s2a(j):
        rs(j, 0).wait_recv()
        part[j, qy, :, :, lo] = (
            part[j, qy, :, :, lo].astype(F32) + d0[j].astype(F32)
        ).astype(BF16)
        rs(j, 4).start()

    def s2b(j):
        rs(j, 2).wait_recv()
        part[j, qx, :, :, hi] = (
            part[j, qx, :, :, hi].astype(F32) + d1[j].astype(F32)
        ).astype(BF16)
        rs(j, 5).start()

    def s3(j, h):
        for i in ((3, 5) if h else (1, 4)):
            rs(j, i).wait_recv()
        c = hi if h else lo
        for i in range(Z - 1):
            zz = z_peers[i] // Q
            sums[j, zz, :, c] = (
                part[j, q, zz, :, c].astype(F32)
                + rx[j, zz, :, c].astype(F32)
                + ry[j, zz, :, c].astype(F32)
            ).astype(BF16)
            rs_z(j, i, h).start()

    def fin(j):
        for h, c in enumerate((lo, hi)):
            for i in range(Z - 1):
                rs_z(j, i, h).wait_recv()
            acc = (
                part[j, q, z, :, c].astype(F32)
                + rx[j, z, :, c].astype(F32)
                + ry[j, z, :, c].astype(F32)
            )
            for i in range(Z - 1):
                acc = acc + zin[j, i, :, c].astype(F32)
            out[j, :, c] = acc.astype(BF16)

    def rs_drain(j):
        for i in range(6):
            rs(j, i).wait_send()
        for i in range(Z - 1):
            rs_z(j, i, 0).wait_send()
            rs_z(j, i, 1).wait_send()

    def crossing():
        return rcopy(out.at[0], late, cross_s, cross_r, me, 1 - sec)

    def tile(n):
        return pl.ds(pl.multiple_of(n * TILE, TILE), TILE)

    def gate_table():
        lane = lax.broadcasted_iota(jnp.int32, (rows, LANES), 1)
        routes = (ra1, rb1, ra2, rb2)
        gates = (ga1, gb1, ga2, gb2)
        acc = jnp.zeros((rows, LANES), F32)
        for j in range(JOBS):
            r = jnp.where(first, routes[j][...], routes[j ^ 1][...]).T
            g = jnp.where(first, gates[j][...], gates[j ^ 1][...]).T
            for k in range(r.shape[1]):
                hit = lane == r[:, k:k + 1] + j * (Q * Z)
                acc = acc + jnp.where(hit, g[:, k:k + 1], 0.0)
        wt[...] = acc

    def column(j):
        lane = lax.broadcasted_iota(jnp.int32, (total, LANES), 1)
        table = gath_w[...].reshape(total, LANES)
        picked = jnp.sum(jnp.where(lane == j * (Q * Z) + me, table, 0.0), axis=1, keepdims=True)
        wcol[...] = jnp.broadcast_to(picked, (total, LANES))

    def a_tile(j, n, is_f):
        @pl.when(is_f)
        def _():
            x = gath[j + (j + 1) // 2].reshape(total, width)
            g = jnp.dot(x, wg[:, tile(n)], preferred_element_type=F32)
            u = jnp.dot(x, wu[:, tile(n)], preferred_element_type=F32)
            h0[:, tile(n)] = (g * jax.nn.sigmoid(g) * u).astype(BF16)

        @pl.when(jnp.logical_not(is_f))
        def _():
            x = gath[jnp.where(j >= 2, 4, j)].reshape(total, width)
            c = gath[j + 1 + j // 3].reshape(total, width)
            g = jnp.dot(x, wg[:, tile(n)], preferred_element_type=F32)
            u = jnp.dot(x, wu[:, tile(n)], preferred_element_type=F32)
            dh = nt_dot(c, wd[tile(n), :])
            sig = jax.nn.sigmoid(g)
            h0[:, tile(n)] = (dh * u * sig * (1.0 + g * (1.0 - sig))).astype(BF16)
            h1[:, tile(n)] = (dh * g * sig).astype(BF16)

    def b_tile(j, n, is_f):
        def put(o):
            w = jnp.concatenate([wcol[...]] * (TILE // LANES), axis=1)
            part[j, :, :, :, tile(n)] = (o * w).astype(BF16).reshape(Q, Z, rows, TILE)

        @pl.when(is_f)
        def _():
            put(jnp.dot(h0[...], wd[:, tile(n)], preferred_element_type=F32))

        @pl.when(jnp.logical_not(is_f))
        def _():
            put(nt_dot(h0[...], wg[tile(n), :]) + nt_dot(h1[...], wu[tile(n), :]))

    def run(*steps):
        def go():
            for fn, *args in steps:
                fn(*args)

        return go

    def cross():
        crossing().start()
        crossing().wait_recv()

    a_tiles = hidden // TILE
    b_tiles = width // TILE
    after_a = {
        (0, 0): run((l1, 3)),
        (0, 1): run((l2, 2)),
        (0, 2): run((start_near, 4), (l1, 4)),
        (1, 0): run((s2a, 0), (s2b, 0)),
        (1, 1): run((l2, 3)),
        (1, 2): run((s3, 0, 0)),
        (2, 0): run((s2a, 1), (s2b, 1)),
        (2, 1): run((l1, 5)),
        (2, 2): run((s3, 1, 0)),
        (3, 0): run((s2a, 2), (s2b, 2)),
        (3, 1): run((s3, 2, 0)),
        (3, 2): run((s3, 2, 1)),
    }
    after_b = {
        (0, 0): run((sa, 0)),
        (0, 1): run((sb, 0), (arrived, 2)),
        (1, 0): run((s3, 0, 1), (sa, 1)),
        (1, 1): run(
            (sb, 1), (l2, 4), (fin, 0), (cross,), (start_z, 5), (start_near, 5),
            (arrived, 3), (arrived, 4),
        ),
        (2, 0): run((l2, 5), (s3, 1, 1), (sa, 2)),
        (2, 1): run((sb, 2), (fin, 1), (arrived, 5)),
        (3, 0): run((sa, 3)),
        (3, 1): run(
            (sb, 3), (s2a, 3), (s2b, 3), (fin, 2), (s3, 3, 0), (s3, 3, 1), (fin, 3)
        ),
    }

    pl.semaphore_wait(barrier, Z + 2)
    start_z(0)
    start_near(0)
    start_z(1)
    start_near(1)
    gate_table()
    start_z(W)
    start_near(W)
    for k in (2, 3, 4):
        start_z(k)
    for c in w_copies:
        c.start()
    l1(0)
    l1(1)
    l1(W)
    l2(0)
    start_near(2)
    l2(1)
    l2(W)
    l1(2)
    start_near(3)
    arrived(0)
    for c in w_copies:
        c.wait()
    arrived(1)
    arrived(W)

    def job(j, carry):
        is_f = (sec + j) % 2 == 0
        column(j)

        def a_step(n, c):
            a_tile(j, n, is_f)
            for (jj, nn), fn in after_a.items():
                at = nn if nn < 2 else a_tiles - 1
                pl.when((j == jj) & (n == at))(fn)
            return c

        lax.fori_loop(0, a_tiles, a_step, 0)

        def b_step(n, c):
            b_tile(j, n, is_f)
            for (jj, nn), fn in after_b.items():
                pl.when((j == jj) & (n == (nn + 1) * (b_tiles // 2) - 1))(fn)
            return c

        lax.fori_loop(0, b_tiles, b_step, 0)
        return carry

    lax.fori_loop(0, JOBS, job, 0)

    for k in range(BIG + 1):
        ag_drain(k)
    for j in range(JOBS):
        rs_drain(j)
    crossing().wait_send()


def fused_shards(
    act_a, route_a1, gate_a1, act_b1, route_b1, gate_b1, grad_b1, act_b2,
    route_a2, gate_a2, route_b2, gate_b2, enter_a, enter_grad, w_gate, w_up, w_down,
):
    experts = lax.axis_size("expert")
    first = lax.axis_index("segment") == 0
    rows, width = act_a.shape[1:]
    hidden = w_gate.shape[3]

    def pick(one, two):
        return jnp.where(first, one, two)

    vmem = pl.BlockSpec(memory_space=pltpu.VMEM)
    hbm = pl.BlockSpec(memory_space=pl.ANY)
    dma = pltpu.SemaphoreType.DMA
    total = experts * rows
    done = pl.pallas_call(
        layer_kernel,
        out_shape=jax.ShapeDtypeStruct((JOBS, rows, width), BF16),
        in_specs=[hbm] * 6 + [vmem] * 8 + [hbm] * 3,
        out_specs=vmem,
        scratch_shapes=[
            pltpu.VMEM((BIG, Q, Z, rows, width), BF16),
            pltpu.VMEM((Q, Z, rows, LANES), F32),
            pltpu.VMEM((rows, LANES), F32),
            pltpu.VMEM((JOBS, Q, Z, rows, width), BF16),
            pltpu.VMEM((rows, width), BF16),
            pltpu.VMEM((width, hidden), BF16),
            pltpu.VMEM((width, hidden), BF16),
            pltpu.VMEM((hidden, width), BF16),
            pltpu.VMEM((total, hidden), BF16),
            pltpu.VMEM((total, hidden), BF16),
            pltpu.VMEM((total, LANES), F32),
            pltpu.VMEM((JOBS, Z, rows, width // 2), BF16),
            pltpu.VMEM((JOBS, Z, rows, width // 2), BF16),
            pltpu.VMEM((JOBS, Z, rows, width), BF16),
            pltpu.VMEM((JOBS, Z, rows, width), BF16),
            pltpu.VMEM((JOBS, Z, rows, width), BF16),
            pltpu.VMEM((JOBS, Z - 1, rows, width), BF16),
            dma((BIG + 1,)), dma((3,)),
            dma((BIG + 1, Z - 1)), dma((BIG + 1, Z - 1)),
            dma((BIG + 1, 2, Z)), dma((BIG + 1, 2, Z)),
            dma((BIG + 1, 2)), dma((BIG + 1, 2)),
            dma((JOBS, 6)), dma((JOBS, 6)),
            dma((JOBS, Z - 1, 2)), dma((JOBS, Z - 1, 2)),
            dma, dma,
        ],
        compiler_params=pltpu.CompilerParams(
            collective_id=0, has_side_effects=True, vmem_limit_bytes=60 * 1024 * 1024
        ),
    )(
        act_a[0], act_b1[0], grad_b1[0], enter_a, enter_grad, act_b2[0],
        route_a1[0].T, route_b1[0].T, route_a2[0].T, route_b2[0].T,
        gate_a1[0].T, gate_b1[0].T, gate_a2[0].T, gate_b2[0].T,
        w_gate[0, 0], w_up[0, 0], w_down[0, 0],
    )
    fwd_one, grad_one = pick(done[0], done[1]), pick(done[1], done[0])
    fwd_two, grad_two = pick(done[2], done[3]), pick(done[3], done[2])
    return (fwd_one[None], grad_one[None], fwd_two[None], grad_two[None])


def solution(mesh):
    split = P("segment", "expert", None)
    weights = P("segment", "expert", None, None)
    in_specs = (split,) * 12 + (P("expert", None),) * 2 + (weights,) * 3
    out_specs = (split,) * 4
    fits = mesh.shape["segment"] == 2 and mesh.shape["expert"] == Q * Z
    body = fused_shards if fits else slot_shards
    return jax.shard_map(body, mesh=mesh, in_specs=in_specs, out_specs=out_specs, check_vma=False)
```

```python
import jax
import jax.numpy as jnp
from jax import lax
from jax.experimental import pallas as pl
from jax.experimental.pallas import tpu as pltpu
from jax.sharding import PartitionSpec as P

TOP = 8


def from_behind(block, axis, distance):
    devices = range(lax.axis_size(axis))
    route = [(i - distance, i) for i in devices if i - distance in devices]
    return lax.ppermute(block, axis, route)


def expert_forward(inputs, gate_mat, up_mat, down_mat):
    gate_pre = jnp.dot(inputs, gate_mat, preferred_element_type=jnp.float32)
    up_pre = jnp.dot(inputs, up_mat, preferred_element_type=jnp.float32)
    hidden = (jax.nn.silu(gate_pre) * up_pre).astype(jnp.bfloat16)
    return jnp.dot(hidden, down_mat, preferred_element_type=jnp.float32).astype(jnp.bfloat16)


def expert_backward(inputs, cotangent, gate_mat, up_mat, down_mat):
    gate_pre = jnp.dot(inputs, gate_mat, preferred_element_type=jnp.float32)
    up_pre = jnp.dot(inputs, up_mat, preferred_element_type=jnp.float32)
    sigma = jax.nn.sigmoid(gate_pre)
    d_hidden = jnp.dot(cotangent, down_mat.T, preferred_element_type=jnp.float32)
    d_gate = (d_hidden * up_pre * sigma * (1.0 + gate_pre * (1.0 - sigma))).astype(jnp.bfloat16)
    d_upper = (d_hidden * gate_pre * sigma).astype(jnp.bfloat16)
    total = jnp.dot(d_gate, gate_mat.T, preferred_element_type=jnp.float32)
    total = total + jnp.dot(d_upper, up_mat.T, preferred_element_type=jnp.float32)
    return total.astype(jnp.bfloat16)


def local_slots(route, capacity, experts):
    routed = route.reshape(-1)
    onehot = (routed[:, None] == jnp.arange(experts, dtype=jnp.int32)[None, :]).astype(jnp.int32)
    before = jnp.cumsum(onehot, axis=0) - onehot
    position = jnp.sum(before * onehot, axis=1)
    return routed * capacity + position


def collect(values, slots, capacity, experts):
    tok_rows = values.shape[0]
    chosen = slots[:, None] == jnp.arange(experts * capacity, dtype=jnp.int32)[None, :]
    select = chosen.reshape(tok_rows, TOP, experts * capacity).any(axis=1).astype(jnp.bfloat16)
    packed = jnp.einsum("tj,td->jd", select, values, preferred_element_type=jnp.float32)
    return packed.astype(jnp.bfloat16).reshape(experts, capacity, values.shape[1])


def spread(returned, slots, gates):
    width = returned.shape[2]
    picked = jnp.take(returned.reshape(-1, width), slots, axis=0).astype(jnp.float32)
    picked = picked.reshape(gates.shape[0], gates.shape[1], width)
    return jnp.sum(picked * gates[:, :, None], axis=1).astype(jnp.bfloat16)


def slot_shards(
    act_a,
    route_a1,
    gate_a1,
    act_b1,
    route_b1,
    gate_b1,
    grad_b1,
    act_b2,
    route_a2,
    gate_a2,
    route_b2,
    gate_b2,
    enter_a,
    enter_grad,
    w_gate,
    w_up,
    w_down,
):
    experts = lax.axis_size("expert")
    tok_rows = act_a.shape[1]
    width = act_a.shape[2]
    capacity = 4 * tok_rows * TOP // (3 * experts)
    gate_mat = w_gate[0, 0]
    up_mat = w_up[0, 0]
    down_mat = w_down[0, 0]

    def run_forward(received):
        flat_in = received.reshape(-1, width)
        return expert_forward(flat_in, gate_mat, up_mat, down_mat).reshape(received.shape)

    def run_backward(received, cot_received):
        flat_in = received.reshape(-1, width)
        flat_cot = cot_received.reshape(-1, width)
        return expert_backward(flat_in, flat_cot, gate_mat, up_mat, down_mat).reshape(
            received.shape
        )

    def one_tick(fwd_in, fwd_route, fwd_gates, bwd_in, bwd_route, bwd_gates, bwd_cot):
        slots_fwd = local_slots(fwd_route, capacity, experts)
        slots_bwd = local_slots(bwd_route, capacity, experts)
        send_fwd = collect(fwd_in, slots_fwd, capacity, experts)
        send_inputs = collect(bwd_in, slots_bwd, capacity, experts)
        send_cot = collect(bwd_cot, slots_bwd, capacity, experts)
        back_fwd = lax.all_to_all(
            run_forward(
                lax.all_to_all(send_fwd, "expert", split_axis=0, concat_axis=0, tiled=True)
            ),
            "expert",
            split_axis=0,
            concat_axis=0,
            tiled=True,
        )
        back_bwd = lax.all_to_all(
            run_backward(
                lax.all_to_all(send_inputs, "expert", split_axis=0, concat_axis=0, tiled=True),
                lax.all_to_all(send_cot, "expert", split_axis=0, concat_axis=0, tiled=True),
            ),
            "expert",
            split_axis=0,
            concat_axis=0,
            tiled=True,
        )
        out_fwd = spread(back_fwd, slots_fwd, fwd_gates)
        out_bwd = spread(back_bwd, slots_bwd, bwd_gates)
        return (out_fwd[None], out_bwd[None])

    fwd_one, grad_one = one_tick(
        act_a[0], route_a1[0], gate_a1[0], act_b1[0], route_b1[0], gate_b1[0], grad_b1[0]
    )
    section = lax.axis_index("segment")
    moved_fwd = from_behind(fwd_one, "segment", 1)
    moved_grad = from_behind(grad_one, "segment", -1)
    in_two = jnp.where(section == 0, enter_a[None], moved_fwd)
    cot_two = jnp.where(section == lax.axis_size("segment") - 1, enter_grad[None], moved_grad)
    fwd_two, grad_two = one_tick(
        in_two[0], route_a2[0], gate_a2[0], act_b2[0], route_b2[0], gate_b2[0], cot_two[0]
    )
    return (fwd_one, grad_one, fwd_two, grad_two)


Z = 4
Q = 4
JOBS = 4
BIG = 6
TILE = 256
LANES = 128
MESH = pl.DeviceIdType.MESH
F32 = jnp.float32
BF16 = jnp.bfloat16


def nt_dot(left, right):
    return lax.dot_general(left, right, (((1,), (1,)), ((), ())), preferred_element_type=F32)


def layer_kernel(
    act_a, act_b1, grad_b1, enter_a, enter_grad, act_b2,
    ra1, rb1, ra2, rb2, ga1, gb1, ga2, gb2, wg_h, wu_h, wd_h, out,
    gath, gath_w, wt, part, late, wg, wu, wd, h0, h1, wcol, d0, d1, rx, ry, sums, zin,
    loc_sem, wsem, agz_s, agz_r, agl_s, agl_r, agd_s, agd_r, rsl_s, rsl_r, rsz_s, rsz_r,
    cross_s, cross_r,
):
    sec = lax.axis_index("segment")
    me = lax.axis_index("expert")
    first = sec == 0
    z = me // Q
    q = me % Q
    x_pos = q % 2
    y_pos = q // 2
    qx = q + 1 - 2 * x_pos
    qy = q + 2 - 4 * y_pos
    qd = Q - 1 - q
    x_peer = z * Q + qx
    y_peer = z * Q + qy
    rows, width = act_a.shape
    total = Q * Z * rows
    half = width // 2
    lo = pl.ds(0, half)
    hi = pl.ds(half, half)
    hidden = wg.shape[1]
    W = BIG

    def rcopy(src, dst, ssem, rsem, peer, seg=sec):
        return pltpu.make_async_remote_copy(
            src_ref=src, dst_ref=dst, send_sem=ssem, recv_sem=rsem,
            device_id=(seg, peer), device_id_type=MESH,
        )

    barrier = pltpu.get_barrier_semaphore()
    z_peers = [((z + j) % Z) * Q + q for j in range(1, Z)]
    z_from = [(z + Z - j) % Z for j in range(1, Z)]
    for peer in z_peers + [x_peer, y_peer]:
        pl.semaphore_signal(barrier, inc=1, device_id=(sec, peer), device_id_type=MESH)
    pl.semaphore_signal(barrier, inc=1, device_id=(1 - sec, me), device_id_type=MESH)

    w_copies = [
        pltpu.make_async_copy(src, dst, wsem.at[i])
        for i, (src, dst) in enumerate(((wg_h, wg), (wu_h, wu), (wd_h, wd)))
    ]

    sources = (
        (act_a, act_b1), (act_b1, grad_b1), (grad_b1, act_a), (enter_a, enter_grad),
        (act_b2, act_b2), (late, late), (wt, wt),
    )

    def by_section(k, fn):
        one, two = sources[k]
        if one is two:
            fn(one)
        else:
            pl.when(first)(lambda: fn(one))
            pl.when(jnp.logical_not(first))(lambda: fn(two))

    def buf(k):
        return gath.at[k] if k < BIG else gath_w

    def own_copy(k, src):
        return pltpu.make_async_copy(src, buf(k).at[q, z], loc_sem.at[k])

    def z_send(k, j, src):
        return rcopy(src, buf(k).at[q, z], agz_s.at[k, j], agz_r.at[k, j], z_peers[j])

    def z_recv(k, j):
        dst = buf(k).at[q, z_from[j]]
        return rcopy(sources[k][0], dst, agz_s.at[k, j], agz_r.at[k, j], z_peers[j])

    def start_z(k):
        def go(src):
            own_copy(k, src).start()
            for j in range(Z - 1):
                z_send(k, j, src).start()

        by_section(k, go)

    def lay(k, axis, i, block, zz, src=None):
        ref = buf(k).at[block, zz]
        peer = x_peer if axis == 0 else y_peer
        return rcopy(
            ref if src is None else src, ref, agl_s.at[k, axis, i], agl_r.at[k, axis, i], peer
        )

    def start_near(k):
        def go(src):
            lay(k, 0, Z - 1, q, z, src).start()
            lay(k, 1, Z - 1, q, z, src).start()

        by_section(k, go)

    def l1(k):
        for j in range(Z - 1):
            z_recv(k, j).wait_recv()
            lay(k, 0, j, q, z_from[j]).start()
            lay(k, 1, j, q, z_from[j]).start()

    def diag(k, i, block):
        if k == W:
            ref = buf(k).at[block]
        else:
            ref = buf(k).at[block, :, :, lo if i == 0 else hi]
        return rcopy(ref, ref, agd_s.at[k, i], agd_r.at[k, i], y_peer if i == 0 else x_peer)

    def near_wait(k, axis):
        block = qx if axis == 0 else qy
        for j in range(Z - 1):
            lay(k, axis, j, block, z_from[j]).wait_recv()
        lay(k, axis, Z - 1, block, z).wait_recv()

    def l2(k):
        near_wait(k, 0)
        diag(k, 0, qx).start()
        near_wait(k, 1)
        if k != W:
            diag(k, 1, qy).start()

    def arrived(k):
        own_copy(k, sources[k][0]).wait()
        diag(k, 0, qd).wait_recv()
        if k != W:
            diag(k, 1, qd).wait_recv()

    def ag_drain(k):
        for j in range(Z - 1):
            z_send(k, j, sources[k][0]).wait_send()
            lay(k, 0, j, q, z_from[j]).wait_send()
            lay(k, 1, j, q, z_from[j]).wait_send()
        lay(k, 0, Z - 1, q, z).wait_send()
        lay(k, 1, Z - 1, q, z).wait_send()
        diag(k, 0, qx).wait_send()
        if k != W:
            diag(k, 1, qy).wait_send()

    quarter = half // 2

    def low(t):
        return pl.ds(t * quarter, quarter)

    def high(t):
        return pl.ds(half + t * quarter, quarter)

    def rs(j, i, t):
        s, d, peer = (
            lambda: (part.at[j, qd, :, :, low(t)], d0.at[j, :, :, low(t)], x_peer),
            lambda: (part.at[j, qx, :, :, low(t)], rx.at[j, :, :, low(t)], x_peer),
            lambda: (part.at[j, qd, :, :, high(t)], d1.at[j, :, :, low(t)], y_peer),
            lambda: (part.at[j, qy, :, :, high(t)], ry.at[j, :, :, high(t)], y_peer),
            lambda: (part.at[j, qy, :, :, low(t)], ry.at[j, :, :, low(t)], y_peer),
            lambda: (part.at[j, qx, :, :, high(t)], rx.at[j, :, :, high(t)], x_peer),
        )[i]()
        return rcopy(s, d, rsl_s.at[j, i, t], rsl_r.at[j, i, t], peer)

    def rs_z(j, i, t, h):
        c = high(t) if h else low(t)
        return rcopy(
            sums.at[j, z_peers[i] // Q, :, c], zin.at[j, i, :, c],
            rsz_s.at[j, i, t, h], rsz_r.at[j, i, t, h], z_peers[i],
        )

    def s1(j, t):
        for i in (0, 2, 1, 3):
            rs(j, i, t).start()

    def s2(j, t):
        rs(j, 0, t).wait_recv()
        part[j, qy, :, :, low(t)] = (
            part[j, qy, :, :, low(t)].astype(F32) + d0[j, :, :, low(t)].astype(F32)
        ).astype(BF16)
        rs(j, 4, t).start()
        rs(j, 2, t).wait_recv()
        part[j, qx, :, :, high(t)] = (
            part[j, qx, :, :, high(t)].astype(F32) + d1[j, :, :, low(t)].astype(F32)
        ).astype(BF16)
        rs(j, 5, t).start()

    def s3(j, t):
        for h, c in enumerate((low(t), high(t))):
            for i in ((3, 5) if h else (1, 4)):
                rs(j, i, t).wait_recv()
            for i in range(Z - 1):
                zz = z_peers[i] // Q
                sums[j, zz, :, c] = (
                    part[j, q, zz, :, c].astype(F32)
                    + rx[j, zz, :, c].astype(F32)
                    + ry[j, zz, :, c].astype(F32)
                ).astype(BF16)
                rs_z(j, i, t, h).start()

    def fin(j):
        for t in range(2):
            for h, c in enumerate((low(t), high(t))):
                for i in range(Z - 1):
                    rs_z(j, i, t, h).wait_recv()
                acc = (
                    part[j, q, z, :, c].astype(F32)
                    + rx[j, z, :, c].astype(F32)
                    + ry[j, z, :, c].astype(F32)
                )
                for i in range(Z - 1):
                    acc = acc + zin[j, i, :, c].astype(F32)
                out[j, :, c] = acc.astype(BF16)

    def rs_drain(j):
        for t in range(2):
            for i in range(6):
                rs(j, i, t).wait_send()
            for i in range(Z - 1):
                rs_z(j, i, t, 0).wait_send()
                rs_z(j, i, t, 1).wait_send()

    def crossing():
        return rcopy(out.at[0], late, cross_s, cross_r, me, 1 - sec)

    def tile(n):
        return pl.ds(pl.multiple_of(n * TILE, TILE), TILE)

    def gate_table():
        lane = lax.broadcasted_iota(jnp.int32, (rows, LANES), 1)
        routes = (ra1, rb1, ra2, rb2)
        gates = (ga1, gb1, ga2, gb2)
        acc = jnp.zeros((rows, LANES), F32)
        for j in range(JOBS):
            r = jnp.where(first, routes[j][...], routes[j ^ 1][...]).T
            g = jnp.where(first, gates[j][...], gates[j ^ 1][...]).T
            for k in range(r.shape[1]):
                hit = lane == r[:, k:k + 1] + j * (Q * Z)
                acc = acc + jnp.where(hit, g[:, k:k + 1], 0.0)
        wt[...] = acc

    def column(j):
        lane = lax.broadcasted_iota(jnp.int32, (total, LANES), 1)
        table = gath_w[...].reshape(total, LANES)
        picked = jnp.sum(jnp.where(lane == j * (Q * Z) + me, table, 0.0), axis=1, keepdims=True)
        wcol[...] = jnp.broadcast_to(picked, (total, LANES))

    def a_tile(j, n, is_f):
        @pl.when(is_f)
        def _():
            x = gath[j + (j + 1) // 2].reshape(total, width)
            g = jnp.dot(x, wg[:, tile(n)], preferred_element_type=F32)
            u = jnp.dot(x, wu[:, tile(n)], preferred_element_type=F32)
            h0[:, tile(n)] = (g * jax.nn.sigmoid(g) * u).astype(BF16)

        @pl.when(jnp.logical_not(is_f))
        def _():
            x = gath[jnp.where(j >= 2, 4, j)].reshape(total, width)
            c = gath[j + 1 + j // 3].reshape(total, width)
            g = jnp.dot(x, wg[:, tile(n)], preferred_element_type=F32)
            u = jnp.dot(x, wu[:, tile(n)], preferred_element_type=F32)
            dh = nt_dot(c, wd[tile(n), :])
            sig = jax.nn.sigmoid(g)
            h0[:, tile(n)] = (dh * u * sig * (1.0 + g * (1.0 - sig))).astype(BF16)
            h1[:, tile(n)] = (dh * g * sig).astype(BF16)

    def b_tile(j, n, is_f):
        def put(o):
            w = jnp.concatenate([wcol[...]] * (TILE // LANES), axis=1)
            part[j, :, :, :, tile(n)] = (o * w).astype(BF16).reshape(Q, Z, rows, TILE)

        @pl.when(is_f)
        def _():
            put(jnp.dot(h0[...], wd[:, tile(n)], preferred_element_type=F32))

        @pl.when(jnp.logical_not(is_f))
        def _():
            put(nt_dot(h0[...], wg[tile(n), :]) + nt_dot(h1[...], wu[tile(n), :]))

    def run(*steps):
        def go():
            for fn, *args in steps:
                fn(*args)

        return go

    def cross():
        crossing().start()
        crossing().wait_recv()

    a_tiles = hidden // TILE
    b_tiles = width // TILE
    after_a = {
        (0, 0): run((l1, 3)),
        (0, 1): run((l2, 2)),
        (0, 2): run((start_near, 4)),
        (1, 0): run((s2, 0, 1), (l2, 3)),
        (1, 1): run((s3, 0, 0)),
        (1, 2): run((s3, 0, 1), (l2, 4)),
        (2, 0): run((s2, 1, 0)),
        (2, 1): run((l1, 5), (s2, 1, 1)),
        (2, 2): run((s3, 1, 0)),
        (3, 0): run((s2, 2, 1)),
        (3, 1): run((s3, 2, 0)),
        (3, 2): run((s3, 2, 1)),
    }
    after_b = {
        (0, 0): run((s1, 0, 0)),
        (0, 1): run((s1, 0, 1), (s2, 0, 0), (l1, 4), (arrived, 2)),
        (1, 0): run((s1, 1, 0), (fin, 0), (cross,), (start_z, 5), (start_near, 5)),
        (1, 1): run((s1, 1, 1), (arrived, 3), (arrived, 4)),
        (2, 0): run((l2, 5), (s3, 1, 1), (s1, 2, 0)),
        (2, 1): run((s1, 2, 1), (fin, 1), (s2, 2, 0), (arrived, 5)),
        (3, 0): run((s1, 3, 0), (fin, 2)),
        (3, 1): run((s1, 3, 1), (s2, 3, 0), (s2, 3, 1), (s3, 3, 0), (s3, 3, 1), (fin, 3)),
    }

    pl.semaphore_wait(barrier, Z + 2)
    start_z(0)
    start_near(0)
    start_z(1)
    start_near(1)
    gate_table()
    start_z(W)
    start_near(W)
    for k in (2, 3, 4):
        start_z(k)
    for c in w_copies:
        c.start()
    l1(0)
    l1(1)
    l1(W)
    l2(0)
    start_near(2)
    l2(1)
    l2(W)
    l1(2)
    start_near(3)
    arrived(0)
    for c in w_copies:
        c.wait()
    arrived(1)
    arrived(W)

    def job(j, carry):
        is_f = (sec + j) % 2 == 0
        column(j)

        def a_step(n, c):
            a_tile(j, n, is_f)
            for (jj, nn), fn in after_a.items():
                at = nn if nn < 2 else a_tiles - 1
                pl.when((j == jj) & (n == at))(fn)
            return c

        lax.fori_loop(0, a_tiles, a_step, 0)

        def b_step(n, c):
            b_tile(j, (n % 2) * (b_tiles // 2) + n // 2, is_f)
            for (jj, nn), fn in after_b.items():
                pl.when((j == jj) & (n == (nn + 1) * (b_tiles // 2) - 1))(fn)
            return c

        lax.fori_loop(0, b_tiles, b_step, 0)
        return carry

    lax.fori_loop(0, JOBS, job, 0)

    for k in range(BIG + 1):
        ag_drain(k)
    for j in range(JOBS):
        rs_drain(j)
    crossing().wait_send()


def fused_shards(
    act_a, route_a1, gate_a1, act_b1, route_b1, gate_b1, grad_b1, act_b2,
    route_a2, gate_a2, route_b2, gate_b2, enter_a, enter_grad, w_gate, w_up, w_down,
):
    experts = lax.axis_size("expert")
    first = lax.axis_index("segment") == 0
    rows, width = act_a.shape[1:]
    hidden = w_gate.shape[3]

    def pick(one, two):
        return jnp.where(first, one, two)

    vmem = pl.BlockSpec(memory_space=pltpu.VMEM)
    hbm = pl.BlockSpec(memory_space=pl.ANY)
    dma = pltpu.SemaphoreType.DMA
    total = experts * rows
    done = pl.pallas_call(
        layer_kernel,
        out_shape=jax.ShapeDtypeStruct((JOBS, rows, width), BF16),
        in_specs=[hbm] * 6 + [vmem] * 8 + [hbm] * 3,
        out_specs=vmem,
        scratch_shapes=[
            pltpu.VMEM((BIG, Q, Z, rows, width), BF16),
            pltpu.VMEM((Q, Z, rows, LANES), F32),
            pltpu.VMEM((rows, LANES), F32),
            pltpu.VMEM((JOBS, Q, Z, rows, width), BF16),
            pltpu.VMEM((rows, width), BF16),
            pltpu.VMEM((width, hidden), BF16),
            pltpu.VMEM((width, hidden), BF16),
            pltpu.VMEM((hidden, width), BF16),
            pltpu.VMEM((total, hidden), BF16),
            pltpu.VMEM((total, hidden), BF16),
            pltpu.VMEM((total, LANES), F32),
            pltpu.VMEM((JOBS, Z, rows, width // 2), BF16),
            pltpu.VMEM((JOBS, Z, rows, width // 2), BF16),
            pltpu.VMEM((JOBS, Z, rows, width), BF16),
            pltpu.VMEM((JOBS, Z, rows, width), BF16),
            pltpu.VMEM((JOBS, Z, rows, width), BF16),
            pltpu.VMEM((JOBS, Z - 1, rows, width), BF16),
            dma((BIG + 1,)), dma((3,)),
            dma((BIG + 1, Z - 1)), dma((BIG + 1, Z - 1)),
            dma((BIG + 1, 2, Z)), dma((BIG + 1, 2, Z)),
            dma((BIG + 1, 2)), dma((BIG + 1, 2)),
            dma((JOBS, 6, 2)), dma((JOBS, 6, 2)),
            dma((JOBS, Z - 1, 2, 2)), dma((JOBS, Z - 1, 2, 2)),
            dma, dma,
        ],
        compiler_params=pltpu.CompilerParams(
            collective_id=0, has_side_effects=True, vmem_limit_bytes=60 * 1024 * 1024
        ),
    )(
        act_a[0], act_b1[0], grad_b1[0], enter_a, enter_grad, act_b2[0],
        route_a1[0].T, route_b1[0].T, route_a2[0].T, route_b2[0].T,
        gate_a1[0].T, gate_b1[0].T, gate_a2[0].T, gate_b2[0].T,
        w_gate[0, 0], w_up[0, 0], w_down[0, 0],
    )
    fwd_one, grad_one = pick(done[0], done[1]), pick(done[1], done[0])
    fwd_two, grad_two = pick(done[2], done[3]), pick(done[3], done[2])
    return (fwd_one[None], grad_one[None], fwd_two[None], grad_two[None])


def solution(mesh):
    split = P("segment", "expert", None)
    weights = P("segment", "expert", None, None)
    in_specs = (split,) * 12 + (P("expert", None),) * 2 + (weights,) * 3
    out_specs = (split,) * 4
    fits = mesh.shape["segment"] == 2 and mesh.shape["expert"] == Q * Z
    body = fused_shards if fits else slot_shards
    return jax.shard_map(body, mesh=mesh, in_specs=in_specs, out_specs=out_specs, check_vma=False)
```
